512 devices in a mesh: tile: 32 (over z, x), node: 16 (over y, core).
Axes of the slice: x: 4, y: 8, z: 8, core: 2. Of those that a mesh axis runs over, the one named last changes fastest.
Arguments:
- features: bfloat16 [262144, 768], P(('tile', 'node')), may hold values from -6 to 6
- target_features: bfloat16 [131072, 768], P(('tile', 'node')), may hold values from -6 to 6
- counts: int32 [512, 2, 6, 256, 256], P(('tile', 'node')), may hold values from 0 to 7
- send_slot: int32 [512, 32, 1], P(('tile', 'node')), may hold values from 0 to 1
- tile_from: int32 [512, 2, 6], P(('tile', 'node')), may hold values from 0 to 31, as said below
- projection: bfloat16 [2304, 768], P('node'), may hold values from -0.125 to 0.125
Outputs:
- projected: bfloat16 [131072, 768], P(('tile', 'node'))
The draws below stay inside these ranges and needn't reach their ends.
Inputs may be any that keep to these rules, and one draw needn't show every extreme that they name: `send_slot`: A local block index of the sending device. `tile_from`: slot q * 1 + c is slot c sent by the device at tile index q in the same node group. The 12 entries of one device name distinct slots where there are that many slots; otherwise every slot is named.
All inputs are finite; a program needn't handle non-finite values.
Results may differ from the reference program's by a relative error of at most 0.0034.
Values may be sent and summed in bfloat16 or wider, within the bound.
No kernel may reach another device: no remote copies, remote signals or barrier semaphores. Data moves between devices by JAX's collectives and lax.ppermute only.
A program may use at most 128 MiB of HBM per device.

```python
import math
import jax
import jax.numpy as jnp
from jax import lax

F = 768
BLK = 256
SB_DEV = 2
TILES_OP = 6
CAP = 1
SOURCES = 262144
TARGETS = 131072
HID = 2304
N_TILE = 32
N_NODE = 16
DEVICES = 512


def draw_tile_from(key, part):
    slot_total = N_TILE * CAP
    device_keys = jax.random.split(jax.random.fold_in(key, 17), DEVICES)
    orders = jax.vmap(lambda single: jax.random.permutation(single, slot_total))(device_keys)
    positions = jnp.arange(2 * TILES_OP, dtype=jnp.int32) % slot_total
    chosen = orders[:, positions].astype(jnp.int32)
    return chosen.reshape(DEVICES, 2, TILES_OP)


def plant(entries, key, smallest, high):
    shape = entries.shape
    place = [jax.random.randint(jax.random.fold_in(key, axis), (), 0, shape[axis]) for axis in range(len(shape))]
    entries = entries.at[tuple(place)].set(smallest)
    longest = shape.index(max(shape))
    place[longest] = (place[longest] + 1) % shape[longest]
    return entries.at[tuple(place)].set(high)


def block_levels(rng, extent, shards, low, top_value):
    gain = 1.0
    for dim, blocks in shards:
        steps = jax.random.uniform(jax.random.fold_in(jax.random.fold_in(rng, 6), dim), (blocks,), jnp.float32, low / len(shards), top_value / len(shards))
        gain = gain * jnp.repeat(jnp.exp(steps), extent[dim] // blocks).reshape((-1,) + (1,) * (len(extent) - 1 - dim))
    return gain


def normal_values(key, shape, scale, reach, shards=(), kind=jnp.bfloat16):
    array = scale * jax.random.normal(key, shape, jnp.float32)
    if shards:
        array = array * block_levels(key, shape, shards, -0.22, 0.18)
    return jnp.clip(array, -reach, reach).astype(kind)


def setup_inputs(seed: int = 0) -> dict:
    key_list = jax.random.split(jax.random.key(seed), 7)
    features = normal_values(key_list[0], (SOURCES, F), 1.0, 6.0, ((0, 512),))
    target_features = normal_values(key_list[1], (TARGETS, F), 1.0, 6.0, ((0, 512),))
    counts = plant(jax.random.randint(key_list[2], (DEVICES, 2, TILES_OP, BLK, BLK), 0, 8), jax.random.fold_in(key_list[2], 1), 0, 7).astype(jnp.int32)
    send_slot = plant(jax.random.randint(key_list[3], (DEVICES, N_TILE, CAP), 0, SB_DEV), jax.random.fold_in(key_list[3], 1), 0, SB_DEV - 1).astype(jnp.int32)
    tile_from = draw_tile_from(jax.random.fold_in(key_list[6], 71), 0)
    projection = normal_values(key_list[5], (HID, F), HID ** -0.5, 0.125, ((0, 16),))
    return dict(features=features, target_features=target_features, counts=counts, send_slot=send_slot, tile_from=tile_from, projection=projection)


def reference(features, target_features, counts, send_slot, tile_from, projection):
    devices = N_TILE * N_NODE
    blocks = features.reshape(devices * SB_DEV, BLK, F)
    scaling = 1.0 / (8.0 * math.sqrt(BLK * TILES_OP))

    def per_target(target):
        tile_pos = target // N_NODE
        node_pos = target % N_NODE
        slot_index = tile_from[target].astype(jnp.int32)
        peer_index = slot_index // CAP
        slot_pos = slot_index % CAP
        source_dev = peer_index * N_NODE + node_pos
        local_block = send_slot[source_dev, tile_pos, slot_pos].astype(jnp.int32)
        block_ids = (source_dev * SB_DEV + local_block).astype(jnp.int32).reshape(-1)
        picked = blocks[block_ids].reshape(2, TILES_OP, BLK, F).astype(jnp.float32)
        tile_weights = counts[target].astype(jnp.float32)
        diffused = jnp.einsum('klts,klsf->ktf', tile_weights, picked) * scaling
        diffused = diffused.astype(jnp.bfloat16)
        own_rows = lax.dynamic_slice_in_dim(target_features, (target * BLK).astype(jnp.int32), BLK, 0)
        stacked = jnp.concatenate([own_rows, diffused[0], diffused[1]], axis=1)
        return jnp.dot(stacked, projection, preferred_element_type=jnp.float32).astype(jnp.bfloat16)
    projected = lax.map(per_target, jnp.arange(devices, dtype=jnp.int32))
    return projected.reshape(devices * BLK, F)
```

```python
import functools
import math

import jax
import jax.numpy as jnp
from jax import lax
from jax.experimental import pallas as pl
from jax.experimental.pallas import tpu as pltpu
from jax.sharding import PartitionSpec as P

NX = 4
NZ = 8
META = 8
LIFT = 2.0**13


def z_groups():
    return [[z * NX + x for z in range(NZ)] for x in range(NX)]


def x_groups():
    return [[z * NX + x for x in range(NX)] for z in range(NZ)]


def sort_kernel(slot_ref, counts_ref, out_ref):
    t = pl.program_id(0)
    rows = counts_ref.shape[-1]
    operator_tiles = pl.num_programs(0) // 2

    @pl.when(t == 0)
    def _():
        out_ref[:, pl.ds(NZ * rows, META), :] = jnp.zeros((NX, META, rows), jnp.bfloat16)

    slot = slot_ref[t]
    z, x = slot // NX, slot % NX
    tile = counts_ref[...].reshape(rows, rows)
    out_ref[x, pl.ds(pl.multiple_of(z * rows, rows), rows), :] = tile.astype(jnp.float32).astype(jnp.bfloat16)
    lane = lax.broadcasted_iota(jnp.int32, (META, rows), 1)
    code = jnp.where(t < operator_tiles, 1.0, 2.0)
    mark = jnp.where(lane == z, code, 0.0)
    old = out_ref[x, pl.ds(NZ * rows, META), :].astype(jnp.float32)
    out_ref[x, pl.ds(NZ * rows, META), :] = (old + mark).astype(jnp.bfloat16)


def sort_tiles(counts, slots):
    tiles, rows = slots.shape[0], counts.shape[-1]
    return pl.pallas_call(
        sort_kernel,
        out_shape=jax.ShapeDtypeStruct((NX, NZ * rows + META, rows), jnp.bfloat16),
        grid_spec=pltpu.PrefetchScalarGridSpec(
            num_scalar_prefetch=1,
            grid=(tiles,),
            in_specs=[pl.BlockSpec((1, rows, rows), lambda t, s: (t, 0, 0))],
            out_specs=pl.BlockSpec((NX, NZ * rows + META, rows), lambda t, s: (0, 0, 0)),
        ),
        name="sort_tiles",
    )(slots, counts.reshape(tiles, rows, rows))


def partial_kernel(scaling, meta_ref, w_ref, f_ref, p_ref, t_ref, sent_ref, own_ref, acc_ref):
    rows, width = t_ref.shape
    x = meta_ref[2 * NX * NZ]

    def diffuse(xd):
        acc_ref[...] = jnp.zeros_like(acc_ref)

        def source(z, carry):
            code = meta_ref[xd * NZ + z]
            block = meta_ref[NX * NZ + xd * NZ + z]

            @pl.when(code > 0)
            def _():
                w = w_ref[xd, pl.ds(pl.multiple_of(z * rows, rows), rows), :]
                f = f_ref[z, pl.ds(pl.multiple_of(block * rows, rows), rows), :]
                acc_ref[code - 1] += jnp.dot(w, f, preferred_element_type=jnp.float32)

            return carry

        lax.fori_loop(0, NZ, source, 0)
        total = None
        for k in range(2):
            d = (acc_ref[k] * scaling).astype(jnp.bfloat16)
            part = jnp.dot(d, p_ref[pl.ds((k + 1) * width, width), :], preferred_element_type=jnp.float32)
            total = part if total is None else total + part
        return total

    def remote(r, carry):
        xd = lax.rem(x + r, NX)
        sent_ref[xd] = diffuse(xd).astype(jnp.bfloat16)
        return carry

    lax.fori_loop(1, NX, remote, 0)
    sent_ref[x] = jnp.zeros((rows, sent_ref.shape[-1]), jnp.bfloat16)
    own_ref[...] = diffuse(x) + jnp.dot(
        t_ref[...], p_ref[pl.ds(0, width), :], preferred_element_type=jnp.float32
    )


def shards(features, target_features, counts, send_slot, tile_from, projection):
    rows, width = counts.shape[-1], features.shape[1]
    out_width = projection.shape[1]
    scaling = 1.0 / (8.0 * math.sqrt(rows * counts.shape[2]))
    me = lax.axis_index("tile")
    my_z, my_x = me // NX, me % NX

    whole_projection = lax.all_gather(projection, "node", axis=0, tiled=True)

    sorted_tiles = sort_tiles(counts, tile_from.reshape(-1))
    tiles = lax.all_to_all(sorted_tiles, "tile", 0, 0, axis_index_groups=x_groups(), tiled=True)

    extra = jnp.pad(send_slot.reshape(1, -1).astype(jnp.float32), ((0, META - 1), (0, width - send_slot.shape[1])))
    payload = jnp.concatenate([features.astype(jnp.float32) * LIFT, extra], axis=0).astype(jnp.float16)
    column = lax.all_gather(payload, "tile", axis=0, tiled=False, axis_index_groups=z_groups())
    blocks = (column[:, :-META].astype(jnp.float32) * (1.0 / LIFT)).astype(jnp.bfloat16)

    picks = lax.dynamic_slice(column[:, -META, :], (0, my_z * NX), (NZ, NX))
    codes = tiles[:, NZ * rows, :NZ]
    meta = jnp.concatenate([
        codes.astype(jnp.int32).reshape(-1),
        picks.astype(jnp.int32).T.reshape(-1),
        my_x.astype(jnp.int32).reshape(1),
    ])
    vmem = pl.BlockSpec(memory_space=pltpu.VMEM)
    sent, own = pl.pallas_call(
        functools.partial(partial_kernel, scaling),
        out_shape=(
            jax.ShapeDtypeStruct((NX, rows, out_width), jnp.bfloat16),
            jax.ShapeDtypeStruct((rows, out_width), jnp.float32),
        ),
        in_specs=[pl.BlockSpec(memory_space=pltpu.SMEM), vmem, vmem, vmem, vmem],
        out_specs=(vmem, vmem),
        scratch_shapes=[pltpu.VMEM((2, rows, width), jnp.float32)],
        name="partial_sums",
    )(meta, tiles, blocks, whole_projection, target_features)
    received = lax.all_to_all(sent, "tile", 0, 0, axis_index_groups=x_groups(), tiled=True)
    return (own + received.astype(jnp.float32).sum(0)).astype(jnp.bfloat16)


def solution(mesh):
    placed = (
        P(("tile", "node"), None),
        P(("tile", "node"), None),
        P(("tile", "node"), None, None, None, None),
        P(("tile", "node"), None, None),
        P(("tile", "node"), None, None),
        P("node", None),
    )
    return jax.shard_map(
        shards, mesh=mesh, in_specs=placed, out_specs=P(("tile", "node"), None), check_vma=False
    )
```
